32 devices in a mesh: dom: 16 (over z, y, x), row: 2 (over core).
Axes of the slice: x: 2, y: 2, z: 4, core: 2. Of those that a mesh axis runs over, the one named last changes fastest.
Arguments:
- features: float32 [4096, 128], P(('dom', 'row')), may hold values from -6 to 6
- history: float32 [4096, 1024], P(('dom', 'row')), may hold values from -3 to 3
- tiles: float32 [32, 4, 128, 128], P(('dom', 'row')), may hold values from -0.25 to 0.25
- tile_cols: int32 [32, 4], P(('dom', 'row')), may hold values from 0 to 1
- cross_weight: float32 [4096, 128], P(('dom', 'row')), may hold values from -0.75 to 0.75
- send_rows: int32 [32, 16, 8], P(('dom', 'row')), may hold values from 0 to 127
- send_count: int32 [32, 16], P(('dom', 'row')), may hold values from 0 to 8, as said below
- cotangent: float32 [4096, 172], P(('dom', 'row')), may hold values from -0.0234375 to 0.0234375
- w_one: float32 [128, 1024], replicated, may hold values from -0.5 to 0.5
- w_two: float32 [1024, 172], replicated, may hold values from -0.1875 to 0.1875
Outputs:
- logits: float32 [4096, 172], P(('dom', 'row'))
- grad_w1: float32 [128, 1024], replicated
- grad_w2: float32 [1024, 172], replicated
The draws below stay inside these ranges and needn't reach their ends.
Inputs may be any that keep to these rules, and one draw needn't show every extreme that they name: send_count is 0 toward the sender's own partition; in every draw some partition receives 8 live rows from every device of every other partition.
All inputs are finite; a program needn't handle non-finite values.
Results may differ from the reference program's by a relative error of at most 0.0003.
Values sent between devices are 32-bit elements; how exact they have to be, the bound alone decides.
A program may use at most 64 MiB of HBM per device.

```python
import jax
import jax.numpy as jnp
from jax import lax

F_IN = 128
HIDDEN_SIZE = 1024
CLASSES = 172
ROWS_DEV = 128
SLOTS = 4
BOUNDARY = 8
PART_ROWS = 256
PART_BLOCKS = 2
NODES = 4096
BLOCKS = 32
N_DOM = 16
N_ROW = 2


def draw_send_count(key, part):
    first_key, second_key = jax.random.split(jax.random.fold_in(key, 7))
    senders = N_DOM * N_ROW
    base_count = jax.random.randint(first_key, (senders, N_DOM), 1, BOUNDARY + 1)
    hot_part = jax.random.randint(second_key, (), 0, N_DOM)
    dest_part = jnp.arange(N_DOM, dtype=jnp.int32)[None, :]
    source_part = (jnp.arange(senders, dtype=jnp.int32) // N_ROW)[:, None]
    counts = jnp.where(dest_part == hot_part, BOUNDARY, base_count)
    counts = jnp.where(dest_part == source_part, 0, counts)
    return counts.astype(jnp.int32)


def place_ends(values, own_key, smallest, high):
    spot = [jax.random.randint(jax.random.fold_in(own_key, axis), (), 0, length) for axis, length in enumerate(values.shape)]
    widest = values.shape.index(max(values.shape))
    neighbour = spot[:widest] + [(spot[widest] + 1) % values.shape[widest]] + spot[widest + 1:]
    return values.at[tuple(spot)].set(smallest).at[tuple(neighbour)].set(high)


def block_scale(key, extent, cuts, least, high):
    level = 1.0
    for position, parts in cuts:
        draws = jax.random.uniform(jax.random.fold_in(jax.random.fold_in(key, 6), position), (parts,), jnp.float32, least / len(cuts), high / len(cuts))
        level = level * jnp.repeat(jnp.exp(draws), extent[position] // parts).reshape((-1,) + (1,) * (len(extent) - 1 - position))
    return level


def centred(stream_key, dims, deviation, reach, cuts=(), kind=jnp.bfloat16):
    result = deviation * jax.random.normal(stream_key, dims, jnp.float32)
    if cuts:
        result = result * block_scale(stream_key, dims, cuts, -0.22, 0.18)
    return jnp.clip(result, -reach, reach).astype(kind)


def setup_inputs(seed: int = 0) -> dict:
    seeds = jax.random.split(jax.random.key(seed), 11)
    features = centred(seeds[0], (NODES, F_IN), 1.0, 6.0, ((0, 32),), jnp.float32)
    history = centred(seeds[1], (NODES, HIDDEN_SIZE), 0.5, 3.0, ((0, 32),), jnp.float32)
    tiles = centred(seeds[2], (BLOCKS, SLOTS, 128, 128), (SLOTS * 128) ** -0.5, 0.25, ((0, 32),), jnp.float32)
    tile_cols = place_ends(jax.random.randint(seeds[3], (BLOCKS, SLOTS), 0, PART_BLOCKS), jax.random.fold_in(seeds[3], 1), 0, PART_BLOCKS - 1).astype(jnp.int32)
    cross_weight = centred(seeds[4], (NODES, N_DOM * BOUNDARY), (N_DOM * BOUNDARY // 2) ** -0.5, 0.75, ((0, 32),), jnp.float32)
    send_rows = place_ends(jax.random.randint(seeds[5], (N_DOM * N_ROW, N_DOM, BOUNDARY), 0, ROWS_DEV), jax.random.fold_in(seeds[5], 1), 0, ROWS_DEV - 1).astype(jnp.int32)
    send_count = draw_send_count(jax.random.fold_in(seeds[10], 71), 0)
    cotangent = centred(seeds[7], (NODES, CLASSES), 0.004, 0.0234375, ((0, 32),), jnp.float32)
    w_one = centred(seeds[8], (F_IN, HIDDEN_SIZE), F_IN ** -0.5, 0.5, (), jnp.float32)
    w_two = centred(seeds[9], (HIDDEN_SIZE, CLASSES), HIDDEN_SIZE ** -0.5, 0.1875, (), jnp.float32)
    return {"features": features, "history": history, "tiles": tiles, "tile_cols": tile_cols, "cross_weight": cross_weight, "send_rows": send_rows, "send_count": send_count, "cotangent": cotangent, "w_one": w_one, "w_two": w_two}


HIGH = lax.Precision.HIGHEST


def gate_act(values):
    sigma = jax.nn.sigmoid(values)
    return values * sigma, sigma * (1.0 + values * (1.0 - sigma))


def reference(features, history, tiles, tile_cols, cross_weight, send_rows, send_count, cotangent, w_one, w_two):
    slot_range = jnp.arange(BOUNDARY, dtype=jnp.int32)
    live_all = (slot_range[None, None, :] < send_count[:, :, None]).astype(jnp.float32)
    lane_index = jnp.arange(128, dtype=jnp.int32)
    senders = jnp.arange(N_DOM * N_ROW, dtype=jnp.int32)

    def one_part(part_index):
        first_row = (part_index * PART_ROWS).astype(jnp.int32)
        first_block = (part_index * PART_BLOCKS).astype(jnp.int32)
        part_feat = lax.dynamic_slice_in_dim(features, first_row, PART_ROWS, 0)
        part_grads = lax.dynamic_slice_in_dim(cotangent, first_row, PART_ROWS, 0)
        tile_part = lax.dynamic_slice_in_dim(tiles, first_block, PART_BLOCKS, 0)
        cols_part = lax.dynamic_slice_in_dim(tile_cols, first_block, PART_BLOCKS, 0)
        cross_part = lax.dynamic_slice_in_dim(cross_weight, first_row, PART_ROWS, 0).reshape(N_ROW, ROWS_DEV, N_DOM * BOUNDARY)
        rows_in = (cols_part[:, :, None] * 128 + lane_index[None, None, :]).astype(jnp.int32)

        def aggregate(values):
            picked = values[rows_in]
            summed = jnp.einsum('bkij,bkjw->biw', tile_part, picked, precision=HIGH)
            return summed.reshape(PART_ROWS, values.shape[1])

        def aggregate_t(values):
            blocked = values.reshape(PART_BLOCKS, 128, values.shape[1])
            contrib = jnp.einsum('bkij,biw->bkjw', tile_part, blocked, precision=HIGH)
            return jax.ops.segment_sum(contrib.reshape(-1, values.shape[1]), rows_in.reshape(-1), num_segments=PART_ROWS)

        local_rows = send_rows[:, part_index, :]
        live_mask = live_all[:, part_index, :]
        global_rows = (senders[:, None] * ROWS_DEV + local_rows).astype(jnp.int32)

        def cross_sum(source_table):
            received = source_table[global_rows] * live_mask[:, :, None]
            received = received.reshape(N_DOM, N_ROW, BOUNDARY, source_table.shape[1]).transpose(1, 0, 2, 3)
            received = received.reshape(N_ROW, N_DOM * BOUNDARY, source_table.shape[1])
            summed = jnp.einsum('rnj,rjw->rnw', cross_part, received, precision=HIGH)
            return summed.reshape(PART_ROWS, source_table.shape[1])

        cross_feat = cross_sum(features)
        cross_hist = cross_sum(history)
        layer_in = aggregate(part_feat) + cross_feat
        pre_act = jnp.dot(layer_in, w_one, precision=HIGH, preferred_element_type=jnp.float32)
        hidden, slope_gate = gate_act(pre_act)
        projected = jnp.dot(hidden, w_two, precision=HIGH, preferred_element_type=jnp.float32)
        logits = aggregate(projected) + jnp.dot(cross_hist, w_two, precision=HIGH, preferred_element_type=jnp.float32)
        back_grad = aggregate_t(part_grads)
        grad_two = jnp.dot(hidden.T, back_grad, precision=HIGH, preferred_element_type=jnp.float32)
        grad_two = grad_two + jnp.dot(cross_hist.T, part_grads, precision=HIGH, preferred_element_type=jnp.float32)
        grad_pre = jnp.dot(back_grad, w_two.T, precision=HIGH, preferred_element_type=jnp.float32) * slope_gate
        grad_one = jnp.dot(layer_in.T, grad_pre, precision=HIGH, preferred_element_type=jnp.float32)
        return logits, grad_one, grad_two

    logits, grads_one, grads_two = lax.map(one_part, jnp.arange(N_DOM, dtype=jnp.int32))
    return logits.reshape(NODES, CLASSES), jnp.sum(grads_one, axis=0), jnp.sum(grads_two, axis=0)
```

```python
import functools
import math

import jax
import jax.numpy as jnp
from jax import lax
from jax.experimental import pallas as pl
from jax.experimental.pallas import tpu as pltpu
from jax.sharding import PartitionSpec as P

MESH = pl.DeviceIdType.MESH
F32 = jnp.float32
BF16 = jnp.bfloat16
NN = (((1,), (0,)), ((), ()))
NT = (((1,), (1,)), ((), ()))


def split(values):
    high = values.astype(BF16)
    return high, (values - high.astype(F32)).astype(BF16)


def dot(left, right, dims=NN):
    one = functools.partial(lax.dot_general, dimension_numbers=dims, preferred_element_type=F32)
    (lh, ll), (rh, rl) = left, right
    return one(lh, rh) + (one(lh, rl) + one(ll, rh))


def pick(chosen, right):
    one = functools.partial(lax.dot_general, dimension_numbers=NN, preferred_element_type=F32)
    return one(chosen, right[0]) + one(chosen, right[1])


def round_up(value, unit):
    return -(-value // unit) * unit


def factors(length):
    inner = 2 ** int(math.log2(math.isqrt(length)))
    return length // inner, inner


def kernel(
    sizes,
    cols_ref, feat_ref, hist_ref, tiles_ref, cw_ref, rows_ref, count_ref, cot_ref, w1_ref, w2_ref,
    logits_ref, g1_ref, g2_ref,
    cotp, w2p, w2h, w2l, adj, fpack, frecv, hpack, hrecv, wpack, wrecv, panel,
    proj, tsend, trecv, hh, hl, slope, grads, rb1, a1, rb2, a2, rb3, full,
    s_feat, r_feat, s_hist, r_hist, s_back, r_back, s_panel, r_panel, s_proj, r_proj, s_tr, r_tr,
    s_row, r_row, s_in, r_in, s_out, r_out, s_gout, r_gout, s_gin, r_gin, s_grow, r_grow,
):
    D, R, O, I, LB = sizes
    NB = w1_ref.shape[1] // 128
    nb = NB // R
    TR = nb * LB
    IP = TR // I
    OP = IP // O
    slots = rows_ref.shape[0]
    NS = D * slots
    C = cot_ref.shape[0]
    C8 = round_up(C, 8)
    CP = cotp.shape[0]
    F = feat_ref.shape[1]
    H = w1_ref.shape[1]
    d = lax.axis_index("dom")
    r = lax.axis_index("row")
    o = d // I
    i = lax.rem(d, I)
    pending = []

    def at(value, unit):
        return pl.multiple_of(value * unit, unit)

    def remote(src, dst, ss, rs, dom, row):
        return pltpu.make_async_remote_copy(
            src_ref=src, dst_ref=dst, send_sem=ss, recv_sem=rs,
            device_id=(dom, row), device_id_type=MESH)

    barrier = pltpu.get_barrier_semaphore()

    def greet(k, carry):
        pl.semaphore_signal(barrier, inc=1, device_id=(lax.rem(d + k, D), r), device_id_type=MESH)
        return carry

    for k in range(1, R):
        pl.semaphore_signal(barrier, inc=1, device_id=(d, lax.rem(r + k, R)), device_id_type=MESH)
    lax.fori_loop(1, D, greet, 0)

    live = lax.broadcasted_iota(jnp.int32, (slots, D), 0) < count_ref[...]
    wanted = jnp.where(live, rows_ref[...], -1).astype(F32).astype(BF16)
    spread = (lax.broadcasted_iota(jnp.int32, (D, NS), 1) // slots
              == lax.broadcasted_iota(jnp.int32, (D, NS), 0)).astype(F32).astype(BF16)
    wide = lax.dot_general(wanted, spread, NN, preferred_element_type=F32)
    own = (lax.rem(lax.broadcasted_iota(jnp.int32, (slots, NS), 1), slots)
           == lax.broadcasted_iota(jnp.int32, (slots, NS), 0))
    row_of = jnp.sum(jnp.where(own, wide, 0.0), axis=0, keepdims=True)
    node = lax.broadcasted_iota(jnp.int32, (128, NS), 0).astype(F32)
    back_f = (node == row_of).astype(F32)
    back_pick = back_f.astype(BF16)
    send_pick = back_f.T.astype(BF16)

    feat = split(feat_ref[...])
    fpack[...] = pick(send_pick, feat)

    pl.semaphore_wait(barrier, D - 1 + R - 1)

    for k in range(1, R):
        c = remote(feat_ref, panel.at[k], s_panel.at[k], r_panel.at[k], d, lax.rem(r + k, R))
        c.start()
        pending.append(c)

    def boundary(pack, recv, ss, rs):
        def one(k):
            dst = lax.rem(d + k, D)
            return remote(pack.at[pl.ds(at(dst, slots), slots)], recv.at[pl.ds(at(d, slots), slots)],
                          ss.at[k], rs.at[k], dst, r)

        def start():
            def body(k, carry):
                one(k).start()
                return carry
            lax.fori_loop(1, D, body, 0)
            mine = pl.ds(at(d, slots), slots)
            recv[mine, :] = pack[mine, :]

        def arrive():
            def body(k, carry):
                src = lax.rem(d + D - k, D)
                remote(pack.at[pl.ds(at(d, slots), slots)], recv.at[pl.ds(at(src, slots), slots)],
                       ss.at[k], rs.at[k], d, r).wait_recv()
                return carry
            lax.fori_loop(1, D, body, 0)

        def leave():
            def body(k, carry):
                one(k).wait_send()
                return carry
            lax.fori_loop(1, D, body, 0)

        return start, arrive, leave

    feat_start, feat_arrive, feat_leave = boundary(fpack, frecv, s_feat, r_feat)
    hist_start, hist_arrive, hist_leave = boundary(hpack, hrecv, s_hist, r_hist)
    back_start, back_arrive, back_leave = boundary(wpack, wrecv, s_back, r_back)
    feat_start()

    cotp[...] = jnp.zeros_like(cotp)
    cotp[0:C, :] = cot_ref[...]
    cot = split(cotp[...])
    for c in range(R):
        total = jnp.zeros((128, 128), F32)
        for k in range(tiles_ref.shape[0]):
            total = total + jnp.where(cols_ref[0, k] == c, tiles_ref[k], 0.0)
        adj[c] = total

    for k in range(1, R):
        dst = lax.rem(r + k, R)
        tsend[k] = dot(cot, split(adj[dst]))[:C8]
        c = remote(tsend.at[k], trecv.at[k], s_tr.at[k], r_tr.at[k], d, dst)
        c.start()
        pending.append(c)
    tsend[0] = dot(cot, split(adj[r]))[:C8]

    cw = cw_ref[...]
    wpack[...] = dot(split(cw.T), cot, NT)
    back_start()

    w2p[...] = jnp.zeros_like(w2p)
    w2p[0:C, :] = w2_ref[...]
    w2 = split(w2p[...])
    w2h[...] = w2[0]
    w2l[...] = w2[1]
    hist = split(hist_ref[...])
    hh[128:256, :] = hist[0]
    hl[128:256, :] = hist[1]
    hpack[...] = pick(send_pick, split(dot(hist, w2, NT)))
    hist_start()

    layer_in = dot(split(adj[r]), feat)
    for k in range(1, R):
        src = lax.rem(r + R - k, R)
        remote(feat_ref, panel.at[k], s_panel.at[k], r_panel.at[k], d, src).wait_recv()
        layer_in = layer_in + dot(split(adj[src]), split(panel[k]))
    cws = split(cw)
    feat_arrive()
    layer_in = layer_in + dot(cws, split(frecv[...]))
    pre = dot(split(layer_in), split(w1_ref[...]))
    sigma = jax.nn.sigmoid(pre)
    hid = split(pre * sigma)
    slope[...] = sigma * (1.0 + pre * (1.0 - sigma))
    hh[0:128, :] = hid[0]
    hl[0:128, :] = hid[1]
    proj[0] = dot((w2h[...], w2l[...]), (hh[0:128, :], hl[0:128, :]), NT)[:C8]
    for k in range(1, R):
        c = remote(proj.at[0], proj.at[k], s_proj.at[k], r_proj.at[k], d, lax.rem(r + k, R))
        c.start()
        pending.append(c)

    for k in range(1, R):
        remote(tsend.at[k], trecv.at[k], s_tr.at[k], r_tr.at[k], d, r).wait_recv()
    bg_t = tsend[0]
    for k in range(1, R):
        bg_t = bg_t + trecv[k]
    cotp[0:C8, :] = bg_t
    bg = split(cotp[...].T)
    back_arrive()
    hb_t = pick(back_pick, split(wrecv[...])).T[:C8]
    both = split(jnp.concatenate([bg_t, hb_t], axis=1))
    lit = split(layer_in.T)

    def block(lb):
        lanes = pl.ds(at(lb, 128), 128)
        base = at(lb, LB)
        gp = dot(bg, (w2h[:, lanes], w2l[:, lanes])) * slope[:, lanes]
        grads[pl.ds(base, F), :] = dot(lit, split(gp))
        grads[pl.ds(pl.multiple_of(base + F, 8), C8), :] = dot(both, (hh[:, lanes], hl[:, lanes]))
        if LB > F + C8:
            grads[pl.ds(pl.multiple_of(base + F + C8, 8), LB - F - C8), :] = jnp.zeros((LB - F - C8, 128), F32)

    def row_copy(k, j, dst):
        inner_block = lax.rem(i + 1 + j, nb)
        return remote(grads.at[pl.ds(at(dst * nb + inner_block, LB), LB)],
                      rb1.at[k, pl.ds(at(inner_block, LB), LB)],
                      s_row.at[k * nb + j], r_row.at[k * nb + j], d, dst)

    def others(step, carry):
        k = 1 + step // nb
        j = lax.rem(step, nb)
        dst = lax.rem(r + k, R)
        block(dst * nb + lax.rem(i + 1 + j, nb))
        row_copy(k, j, dst).start()
        return carry

    def mine(j, carry):
        block(r * nb + lax.rem(i + 1 + j, nb))
        return carry

    lax.fori_loop(0, (R - 1) * nb, others, 0)
    lax.fori_loop(0, nb, mine, 0)

    def inner_copy(k, t):
        dst = lax.rem(i + k, I)
        oo = lax.rem(o + 1 + t, O)
        return remote(a1.at[pl.ds(at(dst * O + oo, OP), OP)], rb2.at[k, pl.ds(at(oo, OP), OP)],
                      s_in.at[k * O + t], r_in.at[k * O + t], o * I + dst, r)

    def inner_send(k):
        for t in range(O):
            c = inner_copy(k, t)
            c.start()
            pending.append(c)

    for j in range(nb):
        inner_block = lax.rem(i + 1 + j, nb)
        rows = pl.ds(at(inner_block, LB), LB)
        total = grads[pl.ds(at(r * nb + inner_block, LB), LB), :]
        for k in range(1, R):
            row_copy(k, j, r).wait_recv()
            total = total + rb1[k, rows, :]
        a1[rows, :] = total
        if nb == I and j < nb - 1:
            inner_send(j + 1)
    if nb != I:
        for k in range(1, I):
            inner_send(k)

    hist_arrive()
    out = dot(cws, split(hrecv[...])).T[:C8]
    out = out + dot(split(proj[0]), split(adj[r]), NT)
    for k in range(1, R):
        src = lax.rem(r + R - k, R)
        remote(proj.at[0], proj.at[k], s_proj.at[k], r_proj.at[k], d, src).wait_recv()
        out = out + dot(split(proj[k]), split(adj[src]), NT)
    logits_ref[...] = out[:C]

    def spot(row, inner, outer):
        return pl.ds(at((row * I + inner) * O + outer, OP), OP)

    for t in range(O):
        oo = lax.rem(o + 1 + t, O)
        total = a1[pl.ds(at(i * O + oo, OP), OP), :]
        for k in range(1, I):
            inner_copy(k, t).wait_recv()
            total = total + rb2[k, pl.ds(at(oo, OP), OP), :]
        a2[t] = total
        if t < O - 1:
            c = remote(a2.at[t], rb3.at[t], s_out.at[t], r_out.at[t], oo * I + i, r)
            c.start()
            pending.append(c)
    total = a2[O - 1]
    for t in range(O - 1):
        remote(a2.at[t], rb3.at[t], s_out.at[t], r_out.at[t], d, r).wait_recv()
        total = total + rb3[t]
    full[spot(r, i, o), :] = total

    def gather(where, ss, rs, index, dom, row):
        return remote(full.at[where], full.at[where], ss.at[index], rs.at[index], dom, row)

    def launch(*rest):
        c = gather(*rest)
        c.start()
        pending.append(c)

    for k in range(1, O):
        launch(spot(r, i, o), s_gout, r_gout, k, lax.rem(o + k, O) * I + i, r)
    for kk in range(O):
        oo = lax.rem(o + O - kk, O)
        if kk:
            gather(spot(r, i, oo), s_gout, r_gout, kk, d, r).wait_recv()
        for k in range(1, I):
            launch(spot(r, i, oo), s_gin, r_gin, k * O + kk, o * I + lax.rem(i + k, I), r)

    def region(row, inner):
        return pl.ds(at(row * I + inner, IP), IP)

    for k in range(I):
        ii = lax.rem(i + I - k, I)
        if k:
            for kk in range(O):
                oo = lax.rem(o + O - kk, O)
                gather(spot(r, ii, oo), s_gin, r_gin, k * O + kk, d, r).wait_recv()
        for kr in range(1, R):
            launch(region(r, ii), s_grow, r_grow, kr * I + k, d, lax.rem(r + kr, R))
    for k in range(I):
        ii = lax.rem(i + I - k, I)
        for kr in range(1, R):
            src = lax.rem(r + R - kr, R)
            gather(region(src, ii), s_grow, r_grow, kr * I + k, d, r).wait_recv()

    for lb in range(NB):
        g1_ref[:, lb * 128:(lb + 1) * 128] = full[lb * LB:lb * LB + F, :]
        g2_ref[:, lb * 128:(lb + 1) * 128] = full[lb * LB + F:lb * LB + F + C, :]

    for c in pending:
        c.wait_send()

    def row_leave(step, carry):
        k = 1 + step // nb
        row_copy(k, lax.rem(step, nb), lax.rem(r + k, R)).wait_send()
        return carry

    lax.fori_loop(0, (R - 1) * nb, row_leave, 0)
    feat_leave()
    hist_leave()
    back_leave()


def on_device(D, R, features, history, tiles, tile_cols, cross_weight, send_rows, send_count, cotangent, w_one, w_two):
    O, I = factors(D)
    F = features.shape[1]
    H = w_one.shape[1]
    C = w_two.shape[1]
    slots = send_rows.shape[2]
    NS = D * slots
    C8 = round_up(C, 8)
    CP = round_up(C, 128)
    LB = round_up(F + C8, max(D * R, 8))
    NB = H // 128
    T = NB * LB
    TR = T // R
    IP = TR // I
    OP = IP // O
    V = pltpu.VMEM
    dma = pltpu.SemaphoreType.DMA
    scratch = [
        V((CP, 128), F32), V((CP, H), F32), V((CP, H), BF16), V((CP, H), BF16), V((R, 128, 128), F32),
        V((NS, F), F32), V((NS, F), F32), V((NS, CP), F32), V((NS, CP), F32), V((NS, CP), F32), V((NS, CP), F32),
        V((R, 128, F), F32), V((R, C8, 128), F32), V((R, C8, 128), F32), V((R, C8, 128), F32),
        V((256, H), BF16), V((256, H), BF16), V((128, H), F32),
        V((T, 128), F32), V((R, TR, 128), F32), V((TR, 128), F32), V((I, IP, 128), F32),
        V((O, OP, 128), F32), V((O, OP, 128), F32), V((T, 128), F32),
    ]
    for count in (D, D, D, R, R, R, NB, I * O, O, O, I * O, R * I):
        scratch += [dma((count,)), dma((count,))]
    in_vmem = pl.BlockSpec(memory_space=pltpu.VMEM)
    logits, grad_one, grad_two = pl.pallas_call(
        functools.partial(kernel, (D, R, O, I, LB)),
        out_shape=(
            jax.ShapeDtypeStruct((C, 128), F32),
            jax.ShapeDtypeStruct((F, H), F32),
            jax.ShapeDtypeStruct((C, H), F32),
        ),
        in_specs=[pl.BlockSpec(memory_space=pltpu.SMEM)] + [in_vmem] * 9,
        out_specs=(in_vmem, in_vmem, in_vmem),
        scratch_shapes=scratch,
        compiler_params=pltpu.CompilerParams(
            collective_id=0, has_side_effects=True, vmem_limit_bytes=60 * 1024 * 1024),
    )(tile_cols, features, history, tiles[0], cross_weight, send_rows[0].T, send_count, cotangent.T, w_one, w_two.T)
    return logits.T, grad_one, grad_two.T


def solution(mesh):
    both = ("dom", "row")
    placed = (
        P(both, None), P(both, None), P(both, None, None, None), P(both, None), P(both, None),
        P(both, None, None), P(both, None), P(both, None), P(), P(),
    )
    return jax.shard_map(
        functools.partial(on_device, mesh.shape["dom"], mesh.shape["row"]),
        mesh=mesh,
        in_specs=placed,
        out_specs=(P(both, None), P(), P()),
        check_vma=False,
    )
```

```python
import functools
import math

import jax
import jax.numpy as jnp
from jax import lax
from jax.experimental import pallas as pl
from jax.experimental.pallas import tpu as pltpu
from jax.sharding import PartitionSpec as P

MESH = pl.DeviceIdType.MESH
F32 = jnp.float32
BF16 = jnp.bfloat16
NN = (((1,), (0,)), ((), ()))
NT = (((1,), (1,)), ((), ()))


def split(values):
    high = values.astype(BF16)
    return high, (values - high.astype(F32)).astype(BF16)


def dot(left, right, dims=NN):
    one = functools.partial(lax.dot_general, dimension_numbers=dims, preferred_element_type=F32)
    (lh, ll), (rh, rl) = left, right
    return one(lh, rh) + (one(lh, rl) + one(ll, rh))


def pick(chosen, right):
    one = functools.partial(lax.dot_general, dimension_numbers=NN, preferred_element_type=F32)
    return one(chosen, right[0]) + one(chosen, right[1])


def round_up(value, unit):
    return -(-value // unit) * unit


def factors(length):
    inner = 2 ** int(math.log2(math.isqrt(length)))
    return length // inner, inner


def kernel(
    sizes,
    cols_ref, *rest,
):
    sources, rest = rest[:9], rest[9:]
    loaded, rest = rest[3:12], rest[:3] + rest[12:]
    rows_ref, count_ref, feat_ref, tiles_ref, cot_ref, cw_ref, hist_ref, w2_ref, w1_ref = loaded
    (
    logits_ref, g1_ref, g2_ref,
    s_load,
    cotp, w2p, w2h, w2l, adj, fpack, frecv, hpack, hrecv, wpack, wrecv, panel,
    proj, tsend, trecv, hh, hl, slope, grads, rb1, a1, rb2, a2, rb3, full,
    s_feat, r_feat, s_hist, r_hist, s_back, r_back, s_panel, r_panel, s_proj, r_proj, s_tr, r_tr,
    s_row, r_row, s_in, r_in, s_out, r_out, s_gout, r_gout, s_gin, r_gin, s_grow, r_grow,
    ) = rest
    D, R, O, I, LB = sizes
    NB = w1_ref.shape[1] // 128
    nb = NB // R
    TR = nb * LB
    IP = TR // I
    OP = IP // O
    slots = rows_ref.shape[0]
    NS = D * slots
    C = cot_ref.shape[0]
    C8 = round_up(C, 8)
    CP = cotp.shape[0]
    F = feat_ref.shape[1]
    H = w1_ref.shape[1]
    d = lax.axis_index("dom")
    r = lax.axis_index("row")
    o = d // I
    i = lax.rem(d, I)
    pending = []

    def at(value, unit):
        return pl.multiple_of(value * unit, unit)

    def remote(src, dst, ss, rs, dom, row):
        return pltpu.make_async_remote_copy(
            src_ref=src, dst_ref=dst, send_sem=ss, recv_sem=rs,
            device_id=(dom, row), device_id_type=MESH)

    barrier = pltpu.get_barrier_semaphore()

    def greet(k, carry):
        pl.semaphore_signal(barrier, inc=1, device_id=(lax.rem(d + k, D), r), device_id_type=MESH)
        return carry

    for k in range(1, R):
        pl.semaphore_signal(barrier, inc=1, device_id=(d, lax.rem(r + k, R)), device_id_type=MESH)
    loads = [pltpu.make_async_copy(src, dst, s_load.at[n]) for n, (src, dst) in enumerate(zip(sources, loaded))]
    for load in loads:
        load.start()
    lax.fori_loop(1, D, greet, 0)
    for load in loads[:3]:
        load.wait()

    live = lax.broadcasted_iota(jnp.int32, (slots, D), 0) < count_ref[...]
    wanted = jnp.where(live, rows_ref[...], -1).astype(F32).astype(BF16)
    spread = (lax.broadcasted_iota(jnp.int32, (D, NS), 1) // slots
              == lax.broadcasted_iota(jnp.int32, (D, NS), 0)).astype(F32).astype(BF16)
    wide = lax.dot_general(wanted, spread, NN, preferred_element_type=F32)
    own = (lax.rem(lax.broadcasted_iota(jnp.int32, (slots, NS), 1), slots)
           == lax.broadcasted_iota(jnp.int32, (slots, NS), 0))
    row_of = jnp.sum(jnp.where(own, wide, 0.0), axis=0, keepdims=True)
    node = lax.broadcasted_iota(jnp.int32, (128, NS), 0).astype(F32)
    back_f = (node == row_of).astype(F32)
    back_pick = back_f.astype(BF16)
    send_pick = back_f.T.astype(BF16)

    feat = split(feat_ref[...])
    fpack[...] = pick(send_pick, feat)

    def boundary(pack, recv, ss, rs):
        def one(k):
            dst = lax.rem(d + k, D)
            return remote(pack.at[pl.ds(at(dst, slots), slots)], recv.at[pl.ds(at(d, slots), slots)],
                          ss.at[k], rs.at[k], dst, r)

        def start():
            def body(k, carry):
                one(k).start()
                return carry
            lax.fori_loop(1, D, body, 0)
            mine = pl.ds(at(d, slots), slots)
            recv[mine, :] = pack[mine, :]

        def arrive():
            def body(k, carry):
                src = lax.rem(d + D - k, D)
                remote(pack.at[pl.ds(at(d, slots), slots)], recv.at[pl.ds(at(src, slots), slots)],
                       ss.at[k], rs.at[k], d, r).wait_recv()
                return carry
            lax.fori_loop(1, D, body, 0)

        def leave():
            def body(k, carry):
                one(k).wait_send()
                return carry
            lax.fori_loop(1, D, body, 0)

        return start, arrive, leave

    feat_start, feat_arrive, feat_leave = boundary(fpack, frecv, s_feat, r_feat)
    hist_start, hist_arrive, hist_leave = boundary(hpack, hrecv, s_hist, r_hist)
    back_start, back_arrive, back_leave = boundary(wpack, wrecv, s_back, r_back)
    for load in loads[3:]:
        load.wait()
    cotp[...] = jnp.zeros_like(cotp)
    cotp[0:C, :] = cot_ref[...]
    cot = split(cotp[...])
    for c in range(R):
        total = jnp.zeros((128, 128), F32)
        for k in range(tiles_ref.shape[0]):
            total = total + jnp.where(cols_ref[0, k] == c, tiles_ref[k], 0.0)
        adj[c] = total

    for k in range(1, R):
        dst = lax.rem(r + k, R)
        tsend[k] = dot(cot, split(adj[dst]))[:C8]
    tsend[0] = dot(cot, split(adj[r]))[:C8]

    cw = cw_ref[...]
    wpack[...] = dot(split(cw.T), cot, NT)

    w2p[...] = jnp.zeros_like(w2p)
    w2p[0:C, :] = w2_ref[...]
    w2 = split(w2p[...])
    w2h[...] = w2[0]
    w2l[...] = w2[1]
    hist = split(hist_ref[...])
    hh[128:256, :] = hist[0]
    hl[128:256, :] = hist[1]
    hpack[...] = pick(send_pick, split(dot(hist, w2, NT)))

    pl.semaphore_wait(barrier, D - 1 + R - 1)

    for k in range(1, R):
        c = remote(feat_ref, panel.at[k], s_panel.at[k], r_panel.at[k], d, lax.rem(r + k, R))
        c.start()
        pending.append(c)
    feat_start()
    for k in range(1, R):
        c = remote(tsend.at[k], trecv.at[k], s_tr.at[k], r_tr.at[k], d, lax.rem(r + k, R))
        c.start()
        pending.append(c)
    back_start()
    hist_start()
    layer_in = dot(split(adj[r]), feat)

    for k in range(1, R):
        src = lax.rem(r + R - k, R)
        remote(feat_ref, panel.at[k], s_panel.at[k], r_panel.at[k], d, src).wait_recv()
        layer_in = layer_in + dot(split(adj[src]), split(panel[k]))
    cws = split(cw)
    feat_arrive()
    layer_in = layer_in + dot(cws, split(frecv[...]))
    pre = dot(split(layer_in), split(w1_ref[...]))
    sigma = jax.nn.sigmoid(pre)
    hid = split(pre * sigma)
    slope[...] = sigma * (1.0 + pre * (1.0 - sigma))
    hh[0:128, :] = hid[0]
    hl[0:128, :] = hid[1]
    proj[0] = dot((w2h[...], w2l[...]), (hh[0:128, :], hl[0:128, :]), NT)[:C8]
    for k in range(1, R):
        c = remote(proj.at[0], proj.at[k], s_proj.at[k], r_proj.at[k], d, lax.rem(r + k, R))
        c.start()
        pending.append(c)

    for k in range(1, R):
        remote(tsend.at[k], trecv.at[k], s_tr.at[k], r_tr.at[k], d, r).wait_recv()
    bg_t = tsend[0]
    for k in range(1, R):
        bg_t = bg_t + trecv[k]
    cotp[0:C8, :] = bg_t
    bg = split(cotp[...].T)
    back_arrive()
    hb_t = pick(back_pick, split(wrecv[...])).T[:C8]
    both = split(jnp.concatenate([bg_t, hb_t], axis=1))
    lit = split(layer_in.T)

    def block(lb):
        lanes = pl.ds(at(lb, 128), 128)
        base = at(lb, LB)
        gp = dot(bg, (w2h[:, lanes], w2l[:, lanes])) * slope[:, lanes]
        grads[pl.ds(base, F), :] = dot(lit, split(gp))
        grads[pl.ds(pl.multiple_of(base + F, 8), C8), :] = dot(both, (hh[:, lanes], hl[:, lanes]))
        if LB > F + C8:
            grads[pl.ds(pl.multiple_of(base + F + C8, 8), LB - F - C8), :] = jnp.zeros((LB - F - C8, 128), F32)

    bits = I.bit_length() - 1

    def low(e):
        return (e & -e).bit_length() - 1 if e else bits

    order = [e for step in range(bits) for e in sorted(
        (e for e in range(1, I) if low(e) == step), key=lambda e: (low(e & (e - 1)), e))] + [0]

    def flipped(row, e):
        place = i
        for step in range(bits):
            if e >> step & 1:
                mask = 0
                for bit in range(bits):
                    mask = mask + jnp.where(lax.rem(row + step, bits) == bit, 1 << bit, 0)
                place = place + mask * (1 - 2 * lax.rem(i // mask, 2))
        return place

    def lane_block(row, j):
        return flipped(row, order[j]) if nb == I else j

    def row_copy(k, j, dst):
        where = lane_block(dst, j)
        return remote(grads.at[pl.ds(at(dst * nb + where, LB), LB)],
                      rb1.at[k, pl.ds(at(where, LB), LB)],
                      s_row.at[k * nb + j], r_row.at[k * nb + j], d, dst)

    partner = [o * I + flipped(r, 1 << step) for step in range(bits)]
    home = [flipped(r, e) for e in range(I)]

    def sum_piece(e, t):
        oo = lax.rem(o + 1 + t, O)
        total = a1[pl.ds(at(home[e] * O + oo, OP), OP), :]
        for step in range(low(e)):
            slot = e | 1 << step
            remote(a2.at[t], rb2.at[slot, pl.ds(at(oo, OP), OP)], s_in.at[slot * O + t], r_in.at[slot * O + t],
                   d, r).wait_recv()
            total = total + rb2[slot, pl.ds(at(oo, OP), OP), :]
        return total

    def pass_on(e):
        for t in range(O):
            oo = lax.rem(o + 1 + t, O)
            piece = pl.ds(at(home[e] * O + oo, OP), OP)
            if low(e):
                a1[piece, :] = sum_piece(e, t)
            c = remote(a1.at[piece], rb2.at[e, pl.ds(at(oo, OP), OP)], s_in.at[e * O + t], r_in.at[e * O + t],
                       partner[low(e)], r)
            c.start()
            pending.append(c)

    for k in range(1, R):
        dst = lax.rem(r + k, R)
        for j in range(nb):
            block(dst * nb + lane_block(dst, j))
            c = row_copy(k, j, dst)
            c.start()
            pending.append(c)
    for j in range(nb):
        where = lane_block(r, j)
        block(r * nb + where)
        rows = pl.ds(at(where, LB), LB)
        total = grads[pl.ds(at(r * nb + where, LB), LB), :]
        for k in range(1, R):
            row_copy(k, j, r).wait_recv()
            total = total + rb1[k, rows, :]
        a1[rows, :] = total
        if nb == I and low(order[j]) == 0:
            pass_on(order[j])
    for e in order[:-1]:
        if nb != I or low(e):
            pass_on(e)

    hist_arrive()
    out = dot(cws, split(hrecv[...])).T[:C8]
    out = out + dot(split(proj[0]), split(adj[r]), NT)
    for k in range(1, R):
        src = lax.rem(r + R - k, R)
        remote(proj.at[0], proj.at[k], s_proj.at[k], r_proj.at[k], d, src).wait_recv()
        out = out + dot(split(proj[k]), split(adj[src]), NT)
    logits_ref[...] = out[:C]

    def spot(row, inner, outer):
        return pl.ds(at((row * I + inner) * O + outer, OP), OP)

    for t in range(O):
        oo = lax.rem(o + 1 + t, O)
        a2[t] = sum_piece(0, t)
        if t < O - 1:
            c = remote(a2.at[t], rb3.at[t], s_out.at[t], r_out.at[t], oo * I + i, r)
            c.start()
            pending.append(c)
    total = a2[O - 1]
    for t in range(O - 1):
        remote(a2.at[t], rb3.at[t], s_out.at[t], r_out.at[t], d, r).wait_recv()
        total = total + rb3[t]
    full[spot(r, i, o), :] = total

    def gather(where, ss, rs, index, dom, row):
        return remote(full.at[where], full.at[where], ss.at[index], rs.at[index], dom, row)

    def launch(*rest):
        c = gather(*rest)
        c.start()
        pending.append(c)

    for k in range(1, O):
        launch(spot(r, i, o), s_gout, r_gout, k, lax.rem(o + k, O) * I + i, r)

    def region(row, inner):
        return pl.ds(at(row * I + inner, IP), IP)

    def handle(e, kk):
        oo = lax.rem(o + O - kk, O)
        if e:
            gather(spot(r, home[e], oo), s_gin, r_gin, e * O + kk, d, r).wait_recv()
        elif kk:
            gather(spot(r, i, oo), s_gout, r_gout, kk, d, r).wait_recv()
        for step in reversed(range(low(e))):
            launch(spot(r, home[e], oo), s_gin, r_gin, (e | 1 << step) * O + kk, partner[step], r)
        if kk == O - 1:
            for kr in range(1, R):
                launch(region(r, home[e]), s_grow, r_grow, kr * I + e, d, lax.rem(r + kr, R))

    ranked = sorted(range(I), key=lambda e: (e.bit_count(), e))
    for turn in range(O + bits):
        for e in ranked:
            if 0 <= turn - e.bit_count() < O:
                handle(e, turn - e.bit_count())
    for e in ranked:
        for kr in range(1, R):
            src = lax.rem(r + R - kr, R)
            gather(region(src, flipped(src, e)), s_grow, r_grow, kr * I + e, d, r).wait_recv()

    for lb in range(NB):
        g1_ref[:, lb * 128:(lb + 1) * 128] = full[lb * LB:lb * LB + F, :]
        g2_ref[:, lb * 128:(lb + 1) * 128] = full[lb * LB + F:lb * LB + F + C, :]

    for c in pending:
        c.wait_send()

    feat_leave()
    hist_leave()
    back_leave()


def on_device(D, R, features, history, tiles, tile_cols, cross_weight, send_rows, send_count, cotangent, w_one, w_two):
    O, I = factors(D)
    F = features.shape[1]
    H = w_one.shape[1]
    C = w_two.shape[1]
    slots = send_rows.shape[2]
    NS = D * slots
    C8 = round_up(C, 8)
    CP = round_up(C, 128)
    LB = round_up(F + C8, max(D * R, 8))
    NB = H // 128
    T = NB * LB
    TR = T // R
    IP = TR // I
    OP = IP // O
    V = pltpu.VMEM
    dma = pltpu.SemaphoreType.DMA
    scratch = [
        V((CP, 128), F32), V((CP, H), F32), V((CP, H), BF16), V((CP, H), BF16), V((R, 128, 128), F32),
        V((NS, F), F32), V((NS, F), F32), V((NS, CP), F32), V((NS, CP), F32), V((NS, CP), F32), V((NS, CP), F32),
        V((R, 128, F), F32), V((R, C8, 128), F32), V((R, C8, 128), F32), V((R, C8, 128), F32),
        V((256, H), BF16), V((256, H), BF16), V((128, H), F32),
        V((T, 128), F32), V((R, TR, 128), F32), V((TR, 128), F32), V((I, IP, 128), F32),
        V((O, OP, 128), F32), V((O, OP, 128), F32), V((T, 128), F32),
    ]
    for count in (D, D, D, R, R, R, NB, I * O, O, O, I * O, R * I):
        scratch += [dma((count,)), dma((count,))]
    in_vmem = pl.BlockSpec(memory_space=pltpu.VMEM)
    operands = (send_rows[0].T, send_count, features, tiles[0], cotangent.T, cross_weight, history, w_two.T, w_one)
    scratch = [V(x.shape, x.dtype) for x in operands] + [dma((len(operands),))] + scratch
    logits, grad_one, grad_two = pl.pallas_call(
        functools.partial(kernel, (D, R, O, I, LB)),
        out_shape=(
            jax.ShapeDtypeStruct((C, 128), F32),
            jax.ShapeDtypeStruct((F, H), F32),
            jax.ShapeDtypeStruct((C, H), F32),
        ),
        in_specs=[pl.BlockSpec(memory_space=pltpu.SMEM)] + [pl.BlockSpec(memory_space=pl.ANY)] * len(operands),
        out_specs=(in_vmem, in_vmem, in_vmem),
        scratch_shapes=scratch,
        compiler_params=pltpu.CompilerParams(
            collective_id=0, has_side_effects=True, vmem_limit_bytes=60 * 1024 * 1024),
    )(tile_cols, *operands)
    return logits.T, grad_one, grad_two.T


def solution(mesh):
    both = ("dom", "row")
    placed = (
        P(both, None), P(both, None), P(both, None, None, None), P(both, None), P(both, None),
        P(both, None, None), P(both, None), P(both, None), P(), P(),
    )
    return jax.shard_map(
        functools.partial(on_device, mesh.shape["dom"], mesh.shape["row"]),
        mesh=mesh,
        in_specs=placed,
        out_specs=(P(both, None), P(), P()),
        check_vma=False,
    )
```

```python
import functools
import math

import jax
import jax.numpy as jnp
from jax import lax
from jax.experimental import pallas as pl
from jax.experimental.pallas import tpu as pltpu
from jax.sharding import PartitionSpec as P

MESH = pl.DeviceIdType.MESH
F32 = jnp.float32
BF16 = jnp.bfloat16
NN = (((1,), (0,)), ((), ()))
NT = (((1,), (1,)), ((), ()))


def split(values):
    high = values.astype(BF16)
    return high, (values - high.astype(F32)).astype(BF16)


def dot(left, right, dims=NN):
    one = functools.partial(lax.dot_general, dimension_numbers=dims, preferred_element_type=F32)
    (lh, ll), (rh, rl) = left, right
    return one(lh, rh) + (one(lh, rl) + one(ll, rh))


def pick(chosen, right):
    one = functools.partial(lax.dot_general, dimension_numbers=NN, preferred_element_type=F32)
    return one(chosen, right[0]) + one(chosen, right[1])


def round_up(value, unit):
    return -(-value // unit) * unit


def factors(length):
    inner = 2 ** int(math.log2(math.isqrt(length)))
    return length // inner, inner


def kernel(
    sizes,
    cols_ref, *rest,
):
    sources, rest = rest[:9], rest[9:]
    loaded, rest = rest[3:12], rest[:3] + rest[12:]
    rows_ref, count_ref, feat_ref, tiles_ref, cot_ref, cw_ref, hist_ref, w2_ref, w1_ref = loaded
    (
    logits_ref, g1_ref, g2_ref,
    s_load,
    cotp, w2p, w2h, w2l, adj, fpack, frecv, hpack, hrecv, wpack, wrecv, panel,
    proj, tsend, trecv, hh, hl, slope, grads, rb1, a1, rb2, a2, rb3, full,
    s_feat, r_feat, s_hist, r_hist, s_back, r_back, s_panel, r_panel, s_proj, r_proj, s_tr, r_tr,
    s_row, r_row, s_in, r_in, s_out, r_out, s_gout, r_gout, s_gin, r_gin, s_grow, r_grow,
    ) = rest
    D, R, O, I, LB = sizes
    NB = w1_ref.shape[1] // 128
    nb = NB // R
    TR = nb * LB
    IP = TR // I
    OP = IP // O
    slots = rows_ref.shape[0]
    NS = D * slots
    C = cot_ref.shape[0]
    C8 = round_up(C, 8)
    CP = cotp.shape[0]
    F = feat_ref.shape[1]
    H = w1_ref.shape[1]
    d = lax.axis_index("dom")
    r = lax.axis_index("row")
    o = d // I
    i = lax.rem(d, I)
    pending = []

    def at(value, unit):
        return pl.multiple_of(value * unit, unit)

    def remote(src, dst, ss, rs, dom, row):
        return pltpu.make_async_remote_copy(
            src_ref=src, dst_ref=dst, send_sem=ss, recv_sem=rs,
            device_id=(dom, row), device_id_type=MESH)

    barrier = pltpu.get_barrier_semaphore()

    def greet(k, carry):
        pl.semaphore_signal(barrier, inc=1, device_id=(lax.rem(d + k, D), r), device_id_type=MESH)
        return carry

    for k in range(1, R):
        pl.semaphore_signal(barrier, inc=1, device_id=(d, lax.rem(r + k, R)), device_id_type=MESH)
    loads = [pltpu.make_async_copy(src, dst, s_load.at[n]) for n, (src, dst) in enumerate(zip(sources, loaded))]
    for load in loads:
        load.start()
    lax.fori_loop(1, D, greet, 0)
    for load in loads[:3]:
        load.wait()

    live = lax.broadcasted_iota(jnp.int32, (slots, D), 0) < count_ref[...]
    wanted = jnp.where(live, rows_ref[...], -1).astype(F32).astype(BF16)
    spread = (lax.broadcasted_iota(jnp.int32, (D, NS), 1) // slots
              == lax.broadcasted_iota(jnp.int32, (D, NS), 0)).astype(F32).astype(BF16)
    wide = lax.dot_general(wanted, spread, NN, preferred_element_type=F32)
    own = (lax.rem(lax.broadcasted_iota(jnp.int32, (slots, NS), 1), slots)
           == lax.broadcasted_iota(jnp.int32, (slots, NS), 0))
    row_of = jnp.sum(jnp.where(own, wide, 0.0), axis=0, keepdims=True)
    node = lax.broadcasted_iota(jnp.int32, (128, NS), 0).astype(F32)
    back_f = (node == row_of).astype(F32)
    back_pick = back_f.astype(BF16)
    send_pick = back_f.T.astype(BF16)

    feat = split(feat_ref[...])
    fpack[...] = pick(send_pick, feat)

    def boundary(pack, recv, ss, rs):
        def one(k):
            dst = lax.rem(d + k, D)
            return remote(pack.at[pl.ds(at(dst, slots), slots)], recv.at[pl.ds(at(d, slots), slots)],
                          ss.at[k], rs.at[k], dst, r)

        def start():
            def body(k, carry):
                one(k).start()
                return carry
            lax.fori_loop(1, D, body, 0)
            mine = pl.ds(at(d, slots), slots)
            recv[mine, :] = pack[mine, :]

        def arrive():
            def body(k, carry):
                src = lax.rem(d + D - k, D)
                remote(pack.at[pl.ds(at(d, slots), slots)], recv.at[pl.ds(at(src, slots), slots)],
                       ss.at[k], rs.at[k], d, r).wait_recv()
                return carry
            lax.fori_loop(1, D, body, 0)

        def leave():
            def body(k, carry):
                one(k).wait_send()
                return carry
            lax.fori_loop(1, D, body, 0)

        return start, arrive, leave

    feat_start, feat_arrive, feat_leave = boundary(fpack, frecv, s_feat, r_feat)
    hist_start, hist_arrive, hist_leave = boundary(hpack, hrecv, s_hist, r_hist)
    back_start, back_arrive, back_leave = boundary(wpack, wrecv, s_back, r_back)
    for load in loads[3:]:
        load.wait()
    cotp[...] = jnp.zeros_like(cotp)
    cotp[0:C, :] = cot_ref[...]
    cot = split(cotp[...])
    for c in range(R):
        total = jnp.zeros((128, 128), F32)
        for k in range(tiles_ref.shape[0]):
            total = total + jnp.where(cols_ref[0, k] == c, tiles_ref[k], 0.0)
        adj[c] = total

    for k in range(1, R):
        dst = lax.rem(r + k, R)
        tsend[k] = dot(cot, split(adj[dst]))[:C8]
    tsend[0] = dot(cot, split(adj[r]))[:C8]

    cw = cw_ref[...]
    wpack[...] = dot(split(cw.T), cot, NT)

    w2p[...] = jnp.zeros_like(w2p)
    w2p[0:C, :] = w2_ref[...]
    w2 = split(w2p[...])
    w2h[...] = w2[0]
    w2l[...] = w2[1]
    hist = split(hist_ref[...])
    hh[128:256, :] = hist[0]
    hl[128:256, :] = hist[1]
    hpack[...] = pick(send_pick, split(dot(hist, w2, NT)))

    pl.semaphore_wait(barrier, D - 1 + R - 1)

    for k in range(1, R):
        c = remote(feat_ref, panel.at[k], s_panel.at[k], r_panel.at[k], d, lax.rem(r + k, R))
        c.start()
        pending.append(c)
    feat_start()
    for k in range(1, R):
        c = remote(tsend.at[k], trecv.at[k], s_tr.at[k], r_tr.at[k], d, lax.rem(r + k, R))
        c.start()
        pending.append(c)
    layer_in = dot(split(adj[r]), feat)

    for k in range(1, R):
        src = lax.rem(r + R - k, R)
        remote(feat_ref, panel.at[k], s_panel.at[k], r_panel.at[k], d, src).wait_recv()
        layer_in = layer_in + dot(split(adj[src]), split(panel[k]))
    cws = split(cw)
    feat_arrive()
    back_start()
    layer_in = layer_in + dot(cws, split(frecv[...]))
    pre = dot(split(layer_in), split(w1_ref[...]))
    sigma = jax.nn.sigmoid(pre)
    hid = split(pre * sigma)
    slope[...] = sigma * (1.0 + pre * (1.0 - sigma))
    hh[0:128, :] = hid[0]
    hl[0:128, :] = hid[1]
    proj[0] = dot((w2h[...], w2l[...]), (hh[0:128, :], hl[0:128, :]), NT)[:C8]
    for k in range(1, R):
        c = remote(proj.at[0], proj.at[k], s_proj.at[k], r_proj.at[k], d, lax.rem(r + k, R))
        c.start()
        pending.append(c)

    hist_start()

    for k in range(1, R):
        remote(tsend.at[k], trecv.at[k], s_tr.at[k], r_tr.at[k], d, r).wait_recv()
    bg_t = tsend[0]
    for k in range(1, R):
        bg_t = bg_t + trecv[k]
    cotp[0:C8, :] = bg_t
    bg = split(cotp[...].T)
    back_arrive()
    hb_t = pick(back_pick, split(wrecv[...])).T[:C8]
    both = split(jnp.concatenate([bg_t, hb_t], axis=1))
    lit = split(layer_in.T)

    def block(lb):
        lanes = pl.ds(at(lb, 128), 128)
        base = at(lb, LB)
        gp = dot(bg, (w2h[:, lanes], w2l[:, lanes])) * slope[:, lanes]
        grads[pl.ds(base, F), :] = dot(lit, split(gp))
        grads[pl.ds(pl.multiple_of(base + F, 8), C8), :] = dot(both, (hh[:, lanes], hl[:, lanes]))
        if LB > F + C8:
            grads[pl.ds(pl.multiple_of(base + F + C8, 8), LB - F - C8), :] = jnp.zeros((LB - F - C8, 128), F32)

    def row_copy(k, j, dst):
        inner_block = lax.rem(i + 1 + j, nb)
        return remote(grads.at[pl.ds(at(dst * nb + inner_block, LB), LB)],
                      rb1.at[k, pl.ds(at(inner_block, LB), LB)],
                      s_row.at[k * nb + j], r_row.at[k * nb + j], d, dst)

    def others(step, carry):
        k = 1 + step // nb
        j = lax.rem(step, nb)
        dst = lax.rem(r + k, R)
        block(dst * nb + lax.rem(i + 1 + j, nb))
        row_copy(k, j, dst).start()
        return carry

    def mine(j, carry):
        block(r * nb + lax.rem(i + 1 + j, nb))
        return carry

    lax.fori_loop(0, (R - 1) * nb, others, 0)
    lax.fori_loop(0, nb, mine, 0)

    def inner_copy(k, t):
        dst = lax.rem(i + k, I)
        oo = lax.rem(o + 1 + t, O)
        return remote(a1.at[pl.ds(at(dst * O + oo, OP), OP)], rb2.at[k, pl.ds(at(oo, OP), OP)],
                      s_in.at[k * O + t], r_in.at[k * O + t], o * I + dst, r)

    for j in range(nb):
        inner_block = lax.rem(i + 1 + j, nb)
        rows = pl.ds(at(inner_block, LB), LB)
        total = grads[pl.ds(at(r * nb + inner_block, LB), LB), :]
        for k in range(1, R):
            row_copy(k, j, r).wait_recv()
            total = total + rb1[k, rows, :]
        a1[rows, :] = total
    for t in range(O):
        for k in range(1, I):
            c = inner_copy(k, t)
            c.start()
            pending.append(c)

    hist_arrive()
    out = dot(cws, split(hrecv[...])).T[:C8]
    out = out + dot(split(proj[0]), split(adj[r]), NT)
    for k in range(1, R):
        src = lax.rem(r + R - k, R)
        remote(proj.at[0], proj.at[k], s_proj.at[k], r_proj.at[k], d, src).wait_recv()
        out = out + dot(split(proj[k]), split(adj[src]), NT)
    logits_ref[...] = out[:C]

    def spot(row, inner, outer):
        return pl.ds(at((row * I + inner) * O + outer, OP), OP)

    for t in range(O):
        oo = lax.rem(o + 1 + t, O)
        total = a1[pl.ds(at(i * O + oo, OP), OP), :]
        for k in range(1, I):
            inner_copy(k, t).wait_recv()
            total = total + rb2[k, pl.ds(at(oo, OP), OP), :]
        a2[t] = total
        if t < O - 1:
            c = remote(a2.at[t], rb3.at[t], s_out.at[t], r_out.at[t], oo * I + i, r)
            c.start()
            pending.append(c)
    total = a2[O - 1]
    for t in range(O - 1):
        remote(a2.at[t], rb3.at[t], s_out.at[t], r_out.at[t], d, r).wait_recv()
        total = total + rb3[t]
    full[spot(r, i, o), :] = total

    def gather(where, ss, rs, index, dom, row):
        return remote(full.at[where], full.at[where], ss.at[index], rs.at[index], dom, row)

    def launch(*rest):
        c = gather(*rest)
        c.start()
        pending.append(c)

    for k in range(1, O):
        launch(spot(r, i, o), s_gout, r_gout, k, lax.rem(o + k, O) * I + i, r)
    for kk in range(O):
        oo = lax.rem(o + O - kk, O)
        if kk:
            gather(spot(r, i, oo), s_gout, r_gout, kk, d, r).wait_recv()
        for k in range(1, I):
            launch(spot(r, i, oo), s_gin, r_gin, k * O + kk, o * I + lax.rem(i + k, I), r)

    def region(row, inner):
        return pl.ds(at(row * I + inner, IP), IP)

    for k in range(I):
        ii = lax.rem(i + I - k, I)
        if k:
            for kk in range(O):
                oo = lax.rem(o + O - kk, O)
                gather(spot(r, ii, oo), s_gin, r_gin, k * O + kk, d, r).wait_recv()
        for kr in range(1, R):
            launch(region(r, ii), s_grow, r_grow, kr * I + k, d, lax.rem(r + kr, R))
    for k in range(I):
        ii = lax.rem(i + I - k, I)
        for kr in range(1, R):
            src = lax.rem(r + R - kr, R)
            gather(region(src, ii), s_grow, r_grow, kr * I + k, d, r).wait_recv()

    for lb in range(NB):
        g1_ref[:, lb * 128:(lb + 1) * 128] = full[lb * LB:lb * LB + F, :]
        g2_ref[:, lb * 128:(lb + 1) * 128] = full[lb * LB + F:lb * LB + F + C, :]

    for c in pending:
        c.wait_send()

    def row_leave(step, carry):
        k = 1 + step // nb
        row_copy(k, lax.rem(step, nb), lax.rem(r + k, R)).wait_send()
        return carry

    lax.fori_loop(0, (R - 1) * nb, row_leave, 0)
    feat_leave()
    hist_leave()
    back_leave()


def hand_over(*refs):
    given, out, held = refs[0:3], refs[3:6], refs[6:9]
    s_get, s_put = refs[9:]
    gets = [pltpu.make_async_copy(given[n], held[n], s_get.at[n]) for n in range(3)]
    puts = [pltpu.make_async_copy(held[n], out[n], s_put.at[n]) for n in range(3)]
    for get in gets:
        get.start()
    for get, put in zip(gets, puts):
        get.wait()
        put.start()
    for put in puts:
        put.wait()


def on_device(D, R, features, history, tiles, tile_cols, cross_weight, send_rows, send_count, cotangent, w_one, w_two):
    O, I = factors(D)
    F = features.shape[1]
    H = w_one.shape[1]
    C = w_two.shape[1]
    slots = send_rows.shape[2]
    NS = D * slots
    C8 = round_up(C, 8)
    CP = round_up(C, 128)
    LB = round_up(F + C8, max(D * R, 8))
    NB = H // 128
    T = NB * LB
    TR = T // R
    IP = TR // I
    OP = IP // O
    V = pltpu.VMEM
    dma = pltpu.SemaphoreType.DMA
    scratch = [
        V((CP, 128), F32), V((CP, H), F32), V((CP, H), BF16), V((CP, H), BF16), V((R, 128, 128), F32),
        V((NS, F), F32), V((NS, F), F32), V((NS, CP), F32), V((NS, CP), F32), V((NS, CP), F32), V((NS, CP), F32),
        V((R, 128, F), F32), V((R, C8, 128), F32), V((R, C8, 128), F32), V((R, C8, 128), F32),
        V((256, H), BF16), V((256, H), BF16), V((128, H), F32),
        V((T, 128), F32), V((R, TR, 128), F32), V((TR, 128), F32), V((I, IP, 128), F32),
        V((O, OP, 128), F32), V((O, OP, 128), F32), V((T, 128), F32),
    ]
    for count in (D, D, D, R, R, R, NB, I * O, O, O, I * O, R * I):
        scratch += [dma((count,)), dma((count,))]
    in_vmem = pl.BlockSpec(memory_space=pltpu.VMEM)
    operands = (send_rows[0].T, send_count, features, tiles[0], cotangent.T, cross_weight, history, w_two.T, w_one)
    scratch = [V(x.shape, x.dtype) for x in operands] + [dma((len(operands),))] + scratch
    logits, grad_one, grad_two = pl.pallas_call(
        functools.partial(kernel, (D, R, O, I, LB)),
        out_shape=(
            jax.ShapeDtypeStruct((C, 128), F32),
            jax.ShapeDtypeStruct((F, H), F32),
            jax.ShapeDtypeStruct((C, H), F32),
        ),
        in_specs=[pl.BlockSpec(memory_space=pltpu.SMEM)] + [pl.BlockSpec(memory_space=pl.ANY)] * len(operands),
        out_specs=(in_vmem, in_vmem, in_vmem),
        scratch_shapes=scratch,
        compiler_params=pltpu.CompilerParams(
            collective_id=0, has_side_effects=True, vmem_limit_bytes=60 * 1024 * 1024),
    )(tile_cols, *operands)
    results = (logits, grad_one, grad_two)
    anywhere = [pl.BlockSpec(memory_space=pl.ANY)] * 3
    logits, grad_one, grad_two = pl.pallas_call(
        hand_over,
        out_shape=tuple(jax.ShapeDtypeStruct(x.shape, x.dtype) for x in results),
        in_specs=anywhere,
        out_specs=tuple(anywhere),
        scratch_shapes=[V(x.shape, x.dtype) for x in results] + [dma((3,)), dma((3,))],
    )(*results)
    return logits.T, grad_one, grad_two.T


def solution(mesh):
    both = ("dom", "row")
    placed = (
        P(both, None), P(both, None), P(both, None, None, None), P(both, None), P(both, None),
        P(both, None, None), P(both, None), P(both, None), P(), P(),
    )
    return jax.shard_map(
        functools.partial(on_device, mesh.shape["dom"], mesh.shape["row"]),
        mesh=mesh,
        in_specs=placed,
        out_specs=(P(both, None), P(), P()),
        check_vma=False,
    )
```

```python
import functools
import math

import jax
import jax.numpy as jnp
from jax import lax
from jax.experimental import pallas as pl
from jax.experimental.pallas import tpu as pltpu
from jax.sharding import PartitionSpec as P

MESH = pl.DeviceIdType.MESH
F32 = jnp.float32
BF16 = jnp.bfloat16
NN = (((1,), (0,)), ((), ()))
NT = (((1,), (1,)), ((), ()))


def split(values):
    high = values.astype(BF16)
    return high, (values - high.astype(F32)).astype(BF16)


def dot(left, right, dims=NN):
    one = functools.partial(lax.dot_general, dimension_numbers=dims, preferred_element_type=F32)
    (lh, ll), (rh, rl) = left, right
    return one(lh, rh) + (one(lh, rl) + one(ll, rh))


def pick(chosen, right):
    one = functools.partial(lax.dot_general, dimension_numbers=NN, preferred_element_type=F32)
    return one(chosen, right[0]) + one(chosen, right[1])


def round_up(value, unit):
    return -(-value // unit) * unit


def factors(length):
    inner = 2 ** int(math.log2(math.isqrt(length)))
    return length // inner, inner


def kernel(
    sizes,
    cols_ref, *rest,
):
    sources, rest = rest[:9], rest[9:]
    loaded, rest = rest[3:12], rest[:3] + rest[12:]
    rows_ref, count_ref, feat_ref, tiles_ref, cot_ref, cw_ref, hist_ref, w2_ref, w1_ref = loaded
    (
    logits_ref, g1_ref, g2_ref,
    s_load,
    cotp, w2p, w2h, w2l, adj, fpack, frecv, hpack, hrecv, wpack, wrecv, panel,
    proj, tsend, trecv, hh, hl, slope, grads, rb1, a1, rb2, a2, rb3, full,
    s_feat, r_feat, s_hist, r_hist, s_back, r_back, s_panel, r_panel, s_proj, r_proj, s_tr, r_tr,
    s_row, r_row, s_in, r_in, s_out, r_out, s_gout, r_gout, s_gin, r_gin, s_grow, r_grow,
    ) = rest
    D, R, O, I, LB = sizes
    NB = w1_ref.shape[1] // 128
    nb = NB // R
    TR = nb * LB
    IP = TR // I
    OP = IP // O
    slots = rows_ref.shape[0]
    NS = D * slots
    C = cot_ref.shape[0]
    C8 = round_up(C, 8)
    CP = cotp.shape[0]
    F = feat_ref.shape[1]
    H = w1_ref.shape[1]
    d = lax.axis_index("dom")
    r = lax.axis_index("row")
    o = d // I
    i = lax.rem(d, I)
    pending = []

    def at(value, unit):
        return pl.multiple_of(value * unit, unit)

    def remote(src, dst, ss, rs, dom, row):
        return pltpu.make_async_remote_copy(
            src_ref=src, dst_ref=dst, send_sem=ss, recv_sem=rs,
            device_id=(dom, row), device_id_type=MESH)

    barrier = pltpu.get_barrier_semaphore()

    def greet(k, carry):
        pl.semaphore_signal(barrier, inc=1, device_id=(lax.rem(d + k, D), r), device_id_type=MESH)
        return carry

    for k in range(1, R):
        pl.semaphore_signal(barrier, inc=1, device_id=(d, lax.rem(r + k, R)), device_id_type=MESH)
    loads = [pltpu.make_async_copy(src, dst, s_load.at[n]) for n, (src, dst) in enumerate(zip(sources, loaded))]
    for load in loads:
        load.start()
    lax.fori_loop(1, D, greet, 0)
    for load in loads[:3]:
        load.wait()

    live = lax.broadcasted_iota(jnp.int32, (slots, D), 0) < count_ref[...]
    wanted = jnp.where(live, rows_ref[...], -1).astype(F32).astype(BF16)
    spread = (lax.broadcasted_iota(jnp.int32, (D, NS), 1) // slots
              == lax.broadcasted_iota(jnp.int32, (D, NS), 0)).astype(F32).astype(BF16)
    wide = lax.dot_general(wanted, spread, NN, preferred_element_type=F32)
    own = (lax.rem(lax.broadcasted_iota(jnp.int32, (slots, NS), 1), slots)
           == lax.broadcasted_iota(jnp.int32, (slots, NS), 0))
    row_of = jnp.sum(jnp.where(own, wide, 0.0), axis=0, keepdims=True)
    node = lax.broadcasted_iota(jnp.int32, (128, NS), 0).astype(F32)
    back_f = (node == row_of).astype(F32)
    back_pick = back_f.astype(BF16)
    send_pick = back_f.T.astype(BF16)

    feat = split(feat_ref[...])
    fpack[...] = pick(send_pick, feat)

    def boundary(pack, recv, ss, rs):
        def one(k):
            dst = lax.rem(d + k, D)
            return remote(pack.at[pl.ds(at(dst, slots), slots)], recv.at[pl.ds(at(d, slots), slots)],
                          ss.at[k], rs.at[k], dst, r)

        def start():
            def body(k, carry):
                one(k).start()
                return carry
            lax.fori_loop(1, D, body, 0)
            mine = pl.ds(at(d, slots), slots)
            recv[mine, :] = pack[mine, :]

        def arrive():
            def body(k, carry):
                src = lax.rem(d + D - k, D)
                remote(pack.at[pl.ds(at(d, slots), slots)], recv.at[pl.ds(at(src, slots), slots)],
                       ss.at[k], rs.at[k], d, r).wait_recv()
                return carry
            lax.fori_loop(1, D, body, 0)

        def leave():
            def body(k, carry):
                one(k).wait_send()
                return carry
            lax.fori_loop(1, D, body, 0)

        return start, arrive, leave

    feat_start, feat_arrive, feat_leave = boundary(fpack, frecv, s_feat, r_feat)
    hist_start, hist_arrive, hist_leave = boundary(hpack, hrecv, s_hist, r_hist)
    back_start, back_arrive, back_leave = boundary(wpack, wrecv, s_back, r_back)
    pl.semaphore_wait(barrier, D - 1 + R - 1)

    for k in range(1, R):
        c = remote(feat_ref, panel.at[k], s_panel.at[k], r_panel.at[k], d, lax.rem(r + k, R))
        c.start()
        pending.append(c)
    feat_start()

    for load in loads[3:]:
        load.wait()
    cotp[...] = jnp.zeros_like(cotp)
    cotp[0:C, :] = cot_ref[...]
    cot = split(cotp[...])
    for c in range(R):
        total = jnp.zeros((128, 128), F32)
        for k in range(tiles_ref.shape[0]):
            total = total + jnp.where(cols_ref[0, k] == c, tiles_ref[k], 0.0)
        adj[c] = total

    for k in range(1, R):
        dst = lax.rem(r + k, R)
        tsend[k] = dot(cot, split(adj[dst]))[:C8]
        c = remote(tsend.at[k], trecv.at[k], s_tr.at[k], r_tr.at[k], d, dst)
        c.start()
        pending.append(c)
    tsend[0] = dot(cot, split(adj[r]))[:C8]

    cw = cw_ref[...]
    wpack[...] = dot(split(cw.T), cot, NT)
    back_start()

    w2p[...] = jnp.zeros_like(w2p)
    w2p[0:C, :] = w2_ref[...]
    w2 = split(w2p[...])
    w2h[...] = w2[0]
    w2l[...] = w2[1]
    hist = split(hist_ref[...])
    hh[128:256, :] = hist[0]
    hl[128:256, :] = hist[1]
    hpack[...] = pick(send_pick, split(dot(hist, w2, NT)))

    layer_in = dot(split(adj[r]), feat)

    for k in range(1, R):
        src = lax.rem(r + R - k, R)
        remote(feat_ref, panel.at[k], s_panel.at[k], r_panel.at[k], d, src).wait_recv()
        layer_in = layer_in + dot(split(adj[src]), split(panel[k]))
    cws = split(cw)
    feat_arrive()
    layer_in = layer_in + dot(cws, split(frecv[...]))
    pre = dot(split(layer_in), split(w1_ref[...]))
    sigma = jax.nn.sigmoid(pre)
    hid = split(pre * sigma)
    slope[...] = sigma * (1.0 + pre * (1.0 - sigma))
    hh[0:128, :] = hid[0]
    hl[0:128, :] = hid[1]
    proj[0] = dot((w2h[...], w2l[...]), (hh[0:128, :], hl[0:128, :]), NT)[:C8]
    for k in range(1, R):
        c = remote(proj.at[0], proj.at[k], s_proj.at[k], r_proj.at[k], d, lax.rem(r + k, R))
        c.start()
        pending.append(c)

    hist_start()

    for k in range(1, R):
        remote(tsend.at[k], trecv.at[k], s_tr.at[k], r_tr.at[k], d, r).wait_recv()
    bg_t = tsend[0]
    for k in range(1, R):
        bg_t = bg_t + trecv[k]
    cotp[0:C8, :] = bg_t
    bg = split(cotp[...].T)
    back_arrive()
    hb_t = pick(back_pick, split(wrecv[...])).T[:C8]
    both = split(jnp.concatenate([bg_t, hb_t], axis=1))
    lit = split(layer_in.T)

    def block(lb):
        lanes = pl.ds(at(lb, 128), 128)
        base = at(lb, LB)
        gp = dot(bg, (w2h[:, lanes], w2l[:, lanes])) * slope[:, lanes]
        grads[pl.ds(base, F), :] = dot(lit, split(gp))
        grads[pl.ds(pl.multiple_of(base + F, 8), C8), :] = dot(both, (hh[:, lanes], hl[:, lanes]))
        if LB > F + C8:
            grads[pl.ds(pl.multiple_of(base + F + C8, 8), LB - F - C8), :] = jnp.zeros((LB - F - C8, 128), F32)

    def row_copy(k, j, dst):
        inner_block = lax.rem(i + 1 + j, nb)
        return remote(grads.at[pl.ds(at(dst * nb + inner_block, LB), LB)],
                      rb1.at[k, pl.ds(at(inner_block, LB), LB)],
                      s_row.at[k * nb + j], r_row.at[k * nb + j], d, dst)

    def others(step, carry):
        k = 1 + step // nb
        j = lax.rem(step, nb)
        dst = lax.rem(r + k, R)
        block(dst * nb + lax.rem(i + 1 + j, nb))
        row_copy(k, j, dst).start()
        return carry

    def mine(j, carry):
        block(r * nb + lax.rem(i + 1 + j, nb))
        return carry

    lax.fori_loop(0, (R - 1) * nb, others, 0)
    lax.fori_loop(0, nb, mine, 0)

    def inner_copy(k, t):
        dst = lax.rem(i + k, I)
        oo = lax.rem(o + 1 + t, O)
        return remote(a1.at[pl.ds(at(dst * O + oo, OP), OP)], rb2.at[k, pl.ds(at(oo, OP), OP)],
                      s_in.at[k * O + t], r_in.at[k * O + t], o * I + dst, r)

    for j in range(nb):
        inner_block = lax.rem(i + 1 + j, nb)
        rows = pl.ds(at(inner_block, LB), LB)
        total = grads[pl.ds(at(r * nb + inner_block, LB), LB), :]
        for k in range(1, R):
            row_copy(k, j, r).wait_recv()
            total = total + rb1[k, rows, :]
        a1[rows, :] = total
    for t in range(O):
        for k in range(1, I):
            c = inner_copy(k, t)
            c.start()
            pending.append(c)

    hist_arrive()
    out = dot(cws, split(hrecv[...])).T[:C8]
    out = out + dot(split(proj[0]), split(adj[r]), NT)
    for k in range(1, R):
        src = lax.rem(r + R - k, R)
        remote(proj.at[0], proj.at[k], s_proj.at[k], r_proj.at[k], d, src).wait_recv()
        out = out + dot(split(proj[k]), split(adj[src]), NT)
    logits_ref[...] = out[:C]

    def spot(row, inner, outer):
        return pl.ds(at((row * I + inner) * O + outer, OP), OP)

    for t in range(O):
        oo = lax.rem(o + 1 + t, O)
        total = a1[pl.ds(at(i * O + oo, OP), OP), :]
        for k in range(1, I):
            inner_copy(k, t).wait_recv()
            total = total + rb2[k, pl.ds(at(oo, OP), OP), :]
        a2[t] = total
        if t < O - 1:
            c = remote(a2.at[t], rb3.at[t], s_out.at[t], r_out.at[t], oo * I + i, r)
            c.start()
            pending.append(c)
    total = a2[O - 1]
    for t in range(O - 1):
        remote(a2.at[t], rb3.at[t], s_out.at[t], r_out.at[t], d, r).wait_recv()
        total = total + rb3[t]
    full[spot(r, i, o), :] = total

    def gather(where, ss, rs, index, dom, row):
        return remote(full.at[where], full.at[where], ss.at[index], rs.at[index], dom, row)

    def launch(*rest):
        c = gather(*rest)
        c.start()
        pending.append(c)

    for k in range(1, O):
        launch(spot(r, i, o), s_gout, r_gout, k, lax.rem(o + k, O) * I + i, r)
    for kk in range(O):
        oo = lax.rem(o + O - kk, O)
        if kk:
            gather(spot(r, i, oo), s_gout, r_gout, kk, d, r).wait_recv()
        for k in range(1, I):
            launch(spot(r, i, oo), s_gin, r_gin, k * O + kk, o * I + lax.rem(i + k, I), r)

    def region(row, inner):
        return pl.ds(at(row * I + inner, IP), IP)

    for k in range(I):
        ii = lax.rem(i + I - k, I)
        if k:
            for kk in range(O):
                oo = lax.rem(o + O - kk, O)
                gather(spot(r, ii, oo), s_gin, r_gin, k * O + kk, d, r).wait_recv()
        for kr in range(1, R):
            launch(region(r, ii), s_grow, r_grow, kr * I + k, d, lax.rem(r + kr, R))
    for k in range(I):
        ii = lax.rem(i + I - k, I)
        for kr in range(1, R):
            src = lax.rem(r + R - kr, R)
            gather(region(src, ii), s_grow, r_grow, kr * I + k, d, r).wait_recv()

    for lb in range(NB):
        g1_ref[:, lb * 128:(lb + 1) * 128] = full[lb * LB:lb * LB + F, :]
        g2_ref[:, lb * 128:(lb + 1) * 128] = full[lb * LB + F:lb * LB + F + C, :]

    for c in pending:
        c.wait_send()

    def row_leave(step, carry):
        k = 1 + step // nb
        row_copy(k, lax.rem(step, nb), lax.rem(r + k, R)).wait_send()
        return carry

    lax.fori_loop(0, (R - 1) * nb, row_leave, 0)
    feat_leave()
    hist_leave()
    back_leave()


def hand_over(*refs):
    given, out, held = refs[0:3], refs[3:6], refs[6:9]
    s_get, s_put = refs[9:]
    gets = [pltpu.make_async_copy(given[n], held[n], s_get.at[n]) for n in range(3)]
    puts = [pltpu.make_async_copy(held[n], out[n], s_put.at[n]) for n in range(3)]
    for get in gets:
        get.start()
    for get, put in zip(gets, puts):
        get.wait()
        put.start()
    for put in puts:
        put.wait()


def on_device(D, R, features, history, tiles, tile_cols, cross_weight, send_rows, send_count, cotangent, w_one, w_two):
    O, I = factors(D)
    F = features.shape[1]
    H = w_one.shape[1]
    C = w_two.shape[1]
    slots = send_rows.shape[2]
    NS = D * slots
    C8 = round_up(C, 8)
    CP = round_up(C, 128)
    LB = round_up(F + C8, max(D * R, 8))
    NB = H // 128
    T = NB * LB
    TR = T // R
    IP = TR // I
    OP = IP // O
    V = pltpu.VMEM
    dma = pltpu.SemaphoreType.DMA
    scratch = [
        V((CP, 128), F32), V((CP, H), F32), V((CP, H), BF16), V((CP, H), BF16), V((R, 128, 128), F32),
        V((NS, F), F32), V((NS, F), F32), V((NS, CP), F32), V((NS, CP), F32), V((NS, CP), F32), V((NS, CP), F32),
        V((R, 128, F), F32), V((R, C8, 128), F32), V((R, C8, 128), F32), V((R, C8, 128), F32),
        V((256, H), BF16), V((256, H), BF16), V((128, H), F32),
        V((T, 128), F32), V((R, TR, 128), F32), V((TR, 128), F32), V((I, IP, 128), F32),
        V((O, OP, 128), F32), V((O, OP, 128), F32), V((T, 128), F32),
    ]
    for count in (D, D, D, R, R, R, NB, I * O, O, O, I * O, R * I):
        scratch += [dma((count,)), dma((count,))]
    in_vmem = pl.BlockSpec(memory_space=pltpu.VMEM)
    operands = (send_rows[0].T, send_count, features, tiles[0], cotangent.T, cross_weight, history, w_two.T, w_one)
    scratch = [V(x.shape, x.dtype) for x in operands] + [dma((len(operands),))] + scratch
    logits, grad_one, grad_two = pl.pallas_call(
        functools.partial(kernel, (D, R, O, I, LB)),
        out_shape=(
            jax.ShapeDtypeStruct((C, 128), F32),
            jax.ShapeDtypeStruct((F, H), F32),
            jax.ShapeDtypeStruct((C, H), F32),
        ),
        in_specs=[pl.BlockSpec(memory_space=pltpu.SMEM)] + [pl.BlockSpec(memory_space=pl.ANY)] * len(operands),
        out_specs=(in_vmem, in_vmem, in_vmem),
        scratch_shapes=scratch,
        compiler_params=pltpu.CompilerParams(
            collective_id=0, has_side_effects=True, vmem_limit_bytes=60 * 1024 * 1024),
    )(tile_cols, *operands)
    results = (logits, grad_one, grad_two)
    anywhere = [pl.BlockSpec(memory_space=pl.ANY)] * 3
    logits, grad_one, grad_two = pl.pallas_call(
        hand_over,
        out_shape=tuple(jax.ShapeDtypeStruct(x.shape, x.dtype) for x in results),
        in_specs=anywhere,
        out_specs=tuple(anywhere),
        scratch_shapes=[V(x.shape, x.dtype) for x in results] + [dma((3,)), dma((3,))],
    )(*results)
    return logits.T, grad_one, grad_two.T


def solution(mesh):
    both = ("dom", "row")
    placed = (
        P(both, None), P(both, None), P(both, None, None, None), P(both, None), P(both, None),
        P(both, None, None), P(both, None), P(both, None), P(), P(),
    )
    return jax.shard_map(
        functools.partial(on_device, mesh.shape["dom"], mesh.shape["row"]),
        mesh=mesh,
        in_specs=placed,
        out_specs=(P(both, None), P(), P()),
        check_vma=False,
    )
```
